32 devices in a mesh: groups: 2 (over y), ep: 4 (over z), node: 2 (over x), sub: 2 (over core).
Axes of the slice: x: 2, y: 2, z: 4, core: 2. Of those that a mesh axis runs over, the one named last changes fastest.
Arguments:
- quantized: bfloat16 [1024, 4096], P(('groups', 'ep', 'sub'), 'node'), parts along dimension 0, may hold values from -6 to 6
- scales: float32 [1024, 32], P(('groups', 'ep', 'sub'), 'node'), parts along dimension 0, may hold values from 0.5 to 2
- expert_ids: int32 [1024, 2], P(('groups', 'ep', 'sub')), parts along dimension 0, may hold values from 0 to 3, all different within a row; in each aligned block of 64 rows (0 to 63, 64 to 127, ...) at most 64 rows name the same one
- combine_weights: float32 [1024, 2], P(('groups', 'ep', 'sub')), parts along dimension 0, may hold values from 0.2 to 1
- gate_weight: bfloat16 [4, 4096, 2048], P('ep', 'sub', 'node'), may hold values from -0.09375 to 0.09375
- up_weight: bfloat16 [4, 4096, 2048], P('ep', 'sub', 'node'), may hold values from -0.09375 to 0.09375
- down_weight: bfloat16 [4, 2048, 4096], P('ep', 'sub', 'node'), may hold values from -0.125 to 0.125
- cotangent: bfloat16 [1024, 4096], P(('groups', 'ep', 'sub'), 'node'), parts along dimension 0, may hold values from -6 to 6
Outputs:
- layer_out: bfloat16 [1024, 4096], P(('groups', 'ep', 'sub'), 'node'), parts along dimension 0
- grad_tokens: bfloat16 [1024, 4096], P(('groups', 'ep', 'sub'), 'node'), parts along dimension 0
- grad_gates: float32 [1024, 2], P(('groups', 'ep', 'sub')), parts along dimension 0
The draws below stay inside these ranges and needn't reach their ends.
There are 2 independent parts, one for each index of `groups`. The reference program is written for one: setup_inputs(seed, part) draws one part's arguments, and reference() takes and returns one part's arrays. A program takes and returns all parts, laid end to end along the dimension named above; an argument that names none is the same for every part. Nothing has to cross between parts.
Inputs may be any that keep to these rules, and one draw needn't show every extreme that they name: `expert_ids`: each row names 2 different experts. In each aligned block of 64 rows (the tokens of one index of ep and sub) no expert is named more than 64 times, and in every draw some expert is named exactly 64 times in some block.
All inputs are finite; a program needn't handle non-finite values.
Results may differ from the reference program's by a relative error of at most 0.022.
Values may be sent and summed in bfloat16 or wider, within the bound.
No kernel may reach another device: no remote copies, remote signals or barrier semaphores. Data moves between devices by JAX's collectives and lax.ppermute only.
A program may use at most 128 MiB of HBM per device.

```python
import math
import jax
import jax.numpy as jnp
import numpy as np
from jax import lax

D = 4096
FF = 2048
BLOCK = 128
TOP = 2
TOK_DEV = 64
EXPERTS = 4
SHARDS = 2
D_DEV = 2048
FF_DEV = 1024
CAP = 64
SLOTS = 512
TOKENS = 512
N_EP = 4
N_SUB = 2


def block_scale(own_key, extent, pieces, low, largest):
    level, own = 1.0, jax.random.fold_in(own_key, 6)
    for axis_at, blocks in pieces:
        heights = jnp.exp(jax.random.uniform(jax.random.fold_in(own, axis_at), (blocks,), jnp.float32, low / len(pieces), largest / len(pieces)))
        level = level * jnp.repeat(heights, extent[axis_at] // blocks).reshape([-1 if axis == axis_at else 1 for axis in range(len(extent))])
    return level


def deal_out(key, own, number, rows, count, top, most, lean):
    sequence = jax.random.permutation(key, count)
    crowded, common = load_shares(count, rows * top, most, lean, True), load_shares(count, rows * top, most, lean, False)
    places = jnp.arange(count)

    def named(tallies, offset_by):
        used = int((tallies > 0).sum())
        fixed = max(1, used // 4)
        passed = fixed + (places - fixed + offset_by * (used - fixed)) % max(1, count - fixed)
        return jnp.zeros((count,), jnp.int32).at[sequence[jnp.where(places < fixed, places, passed)]].set(jnp.asarray(tallies, jnp.int32))

    tallies = jnp.where(number % 4 == 0, named(crowded, number // 4), named(common, number - number // 4 - 1))
    mixed = jax.random.permutation(jax.random.fold_in(own, 3), count)
    source_of, receiver = mixed[0:count // 2 * 2:2], mixed[1:count // 2 * 2:2]
    room = jnp.minimum(tallies[source_of] - 1, most - tallies[receiver]) // 2
    room = jnp.where((source_of == sequence[0]) | (receiver == sequence[0]) | (tallies[receiver] == 0), 0, jnp.maximum(room, 0))
    passed = jax.random.randint(jax.random.fold_in(own, 4), (count // 2,), 0, 1 << 20) % (room + 1)
    tallies = tallies.at[source_of].add(-passed).at[receiver].add(passed)
    members = jnp.searchsorted(jnp.cumsum(tallies), jnp.arange(rows * top), side="right").astype(jnp.int32)
    grid = members.reshape(top, rows).T
    grid = grid[jax.random.permutation(jax.random.fold_in(own, 1), rows)]
    offset_by = jax.random.randint(jax.random.fold_in(own, 2), (rows, 1), 0, top)
    return jnp.take_along_axis(grid, (jnp.arange(top)[None, :] + offset_by) % top, axis=1)


def load_shares(count, total, most, slope, full):
    portions = [(1 << 20) // math.isqrt(standing ** slope) + 1 for standing in range(1, count + 1)]
    largest = most if full else min(most, max(-(-total // count), total * portions[0] // sum(portions)))
    least = 1 if total - largest >= count - 1 else 0
    holding, rest = [largest] + [least] * (count - 1), total - largest - least * (count - 1)
    while rest > 0:
        movable = [i for i in range(1, count) if holding[i] < largest] or [i for i in range(1, count) if holding[i] < most]
        whole, budget = sum([portions[i] for i in movable]), rest
        for i in movable:
            more = min(most - holding[i], max(1, budget * portions[i] // whole), rest)
            holding[i] = holding[i] + more
            rest = rest - more
    return np.array(holding)


def gaussian(key, shape, width, limit, split=(), held_as=jnp.bfloat16):
    loudness = block_scale(key, shape, split, -0.22, 0.18) if split else 1.0
    entries = jax.random.normal(key, shape, jnp.float32) * width * loudness
    return jnp.minimum(jnp.maximum(entries, -limit), limit).astype(held_as)


def setup_inputs(seed: int = 0, part: int = 0) -> dict:
    arg_keys = jax.random.split(jax.random.key(seed), 9)
    part_keys = jax.random.split(jax.random.fold_in(arg_keys[8], part), 9)
    quantized = gaussian(part_keys[0], (TOKENS, D), 1.0, 6.0, ((0, 8), (1, 2)))
    scales = jnp.clip(jnp.exp(math.log(2.0) - 1.3862944 * jax.random.uniform(part_keys[1], (TOKENS, D // BLOCK), jnp.float32) ** block_scale(part_keys[1], (TOKENS, D // BLOCK), ((0, 8), (1, 2)), -0.2, 0.2)), 0.5, 2.0)
    expert_ids_keys = jax.random.split(jax.random.fold_in(part_keys[2], 1), TOKENS // TOK_DEV)
    expert_ids_turns = jax.random.permutation(jax.random.fold_in(part_keys[2], 3), TOKENS // TOK_DEV)
    expert_ids = jax.vmap(lambda own, number: deal_out(jax.random.fold_in(part_keys[2], 2), own, number, TOK_DEV, EXPERTS, TOP, CAP, 2))(expert_ids_keys, expert_ids_turns).reshape((TOKENS, TOP))
    combine_weights = jnp.clip(0.2 + 0.8 * jax.random.uniform(part_keys[3], (TOKENS, TOP), jnp.float32) ** block_scale(part_keys[3], (TOKENS, TOP), ((0, 8),), -0.2, 0.2), 0.2, 1.0)
    gate_weight = gaussian(arg_keys[4], (EXPERTS, D, FF), D ** -0.5, 0.09375, ((0, 4), (1, 2), (2, 2)))
    up_weight = gaussian(arg_keys[5], (EXPERTS, D, FF), D ** -0.5, 0.09375, ((0, 4), (1, 2), (2, 2)))
    down_weight = gaussian(arg_keys[6], (EXPERTS, FF, D), FF ** -0.5, 0.125, ((0, 4), (1, 2), (2, 2)))
    cotangent = gaussian(part_keys[7], (TOKENS, D), 1.0, 6.0, ((0, 8), (1, 2)))
    return dict(quantized=quantized, scales=scales, expert_ids=expert_ids, combine_weights=combine_weights, gate_weight=gate_weight, up_weight=up_weight, down_weight=down_weight, cotangent=cotangent)


def silu_parts(values):
    logistic = jax.nn.sigmoid(values)
    return values * logistic, logistic * (1.0 + values * (1.0 - logistic))


def reference(quantized, scales, expert_ids, combine_weights, gate_weight, up_weight, down_weight, cotangent):
    widened = jnp.repeat(scales, BLOCK, axis=1)
    tokens = (quantized.astype(jnp.float32) * widened).astype(jnp.bfloat16)
    onehot = (expert_ids.reshape(N_EP * N_SUB, TOK_DEV * TOP, 1) == jnp.arange(EXPERTS, dtype=jnp.int32)).astype(jnp.int32)
    before = jnp.cumsum(onehot, axis=1) - onehot
    slot_index = jnp.sum(before * onehot, axis=2).reshape(TOKENS, TOP).astype(jnp.int32)
    source = (jnp.arange(TOKENS, dtype=jnp.int32) // TOK_DEV)[:, None]
    target_row = (source * CAP + slot_index).astype(jnp.int32)
    token_index = jnp.broadcast_to(jnp.arange(TOKENS, dtype=jnp.int32)[:, None], (TOKENS, TOP))
    expert_rows = jnp.zeros((EXPERTS, SLOTS, D), jnp.bfloat16).at[expert_ids, target_row].set(tokens[token_index])
    scaled = (combine_weights[:, :, None] * cotangent.astype(jnp.float32)[:, None, :]).astype(jnp.bfloat16)
    cotangent_rows = jnp.zeros((EXPERTS, SLOTS, D), jnp.bfloat16).at[expert_ids, target_row].set(scaled)

    def expert_pass(operands):
        rows_in, grad_in, weight_gate, weight_up, weight_down = operands
        gate_pre = jnp.dot(rows_in, weight_gate, preferred_element_type=jnp.float32)
        up_pre = jnp.dot(rows_in, weight_up, preferred_element_type=jnp.float32)
        activated, derivative = silu_parts(gate_pre)
        hidden = (activated * up_pre).astype(jnp.bfloat16)
        output_rows = jnp.dot(hidden, weight_down, preferred_element_type=jnp.float32).astype(jnp.bfloat16)
        grad_blocks = grad_in.reshape(SLOTS, SHARDS, D_DEV).astype(jnp.float32)
        down_blocks = weight_down.reshape(FF, SHARDS, D_DEV).astype(jnp.float32)
        partial_value = jnp.einsum("rjd,fjd->jrf", grad_blocks, down_blocks)
        rounded = lax.optimization_barrier(partial_value.astype(jnp.bfloat16))
        hidden_grad = jnp.sum(rounded.astype(jnp.float32), axis=0)
        gate_grad = (hidden_grad * up_pre * derivative).astype(jnp.bfloat16)
        up_grad = (hidden_grad * activated).astype(jnp.bfloat16)
        gate_blocks = gate_grad.reshape(SLOTS, SHARDS, FF_DEV).astype(jnp.float32)
        up_blocks = up_grad.reshape(SLOTS, SHARDS, FF_DEV).astype(jnp.float32)
        gate_tiles = weight_gate.reshape(D, SHARDS, FF_DEV).astype(jnp.float32)
        up_tiles = weight_up.reshape(D, SHARDS, FF_DEV).astype(jnp.float32)
        input_part = jnp.einsum("rjh,djh->jrd", gate_blocks, gate_tiles)
        input_part = input_part + jnp.einsum("rjh,djh->jrd", up_blocks, up_tiles)
        rounded_input = lax.optimization_barrier(input_part.astype(jnp.bfloat16))
        input_rows = jnp.sum(rounded_input.astype(jnp.float32), axis=0).astype(jnp.bfloat16)
        return output_rows, input_rows

    output_rows, input_rows = lax.map(expert_pass, (expert_rows, cotangent_rows, gate_weight, up_weight, down_weight))
    picked = output_rows[expert_ids, target_row].astype(jnp.float32)
    layer_out = jnp.sum(combine_weights[:, :, None] * picked, axis=1).astype(jnp.bfloat16)
    grad_gates = jnp.sum(cotangent.astype(jnp.float32)[:, None, :] * picked, axis=2)
    grad_tokens = jnp.sum(input_rows[expert_ids, target_row].astype(jnp.float32), axis=1).astype(jnp.bfloat16)
    return layer_out, grad_tokens, grad_gates
```

```python
import jax
import jax.numpy as jnp
from jax import lax
from jax.sharding import PartitionSpec as P

BLOCK = 128
BF16 = jnp.bfloat16
F32 = jnp.float32
BACK_DIMS = (((1,), (1,)), ((), ()))


def slotted(
    quantized, scales, expert_ids, combine_weights, gate_weight, up_weight, down_weight, cotangent
):
    ep_count = lax.axis_size("ep")
    tok_count, top_count = expert_ids.shape
    width_dev = quantized.shape[1]
    capacity = 2 * tok_count * top_count // ep_count
    row_count = ep_count * capacity
    widened = jnp.repeat(scales, BLOCK, axis=1)
    tokens = (quantized.astype(F32) * widened).astype(BF16)
    onehot = (expert_ids.reshape(-1, 1) == jnp.arange(ep_count, dtype=jnp.int32)).astype(jnp.int32)
    before = jnp.cumsum(onehot, axis=0) - onehot
    slot_index = jnp.sum(before * onehot, axis=1)
    target_row = (expert_ids.reshape(-1) * capacity + slot_index).reshape(tok_count, top_count)
    matches = target_row[:, :, None] == jnp.arange(row_count, dtype=jnp.int32)
    route_map = jnp.any(matches, axis=1)
    slot_weight = jnp.sum(jnp.where(matches, combine_weights[:, :, None], 0.0), axis=(0, 1))
    spread = route_map.astype(BF16)
    dispatch_dims = (((0,), (0,)), ((), ()))
    buffer = lax.dot_general(
        spread, tokens, dispatch_dims, preferred_element_type=F32
    ).astype(BF16)
    moved_grad = lax.dot_general(spread, cotangent, dispatch_dims, preferred_element_type=F32)
    weighted = (moved_grad * slot_weight[:, None]).astype(BF16)
    gate_local, up_local, down_local = (
        lax.all_gather(gate_weight[0], "sub", axis=0, tiled=True),
        lax.all_gather(up_weight[0], "sub", axis=0, tiled=True),
        lax.all_gather(down_weight[0], "sub", axis=0, tiled=True),
    )

    def exchange(rows):
        return lax.all_to_all(
            rows.reshape(ep_count, capacity, width_dev), "ep", split_axis=0, concat_axis=0, tiled=True
        ).reshape(row_count, width_dev)

    portion = lax.all_gather(exchange(buffer), "node", axis=1, tiled=True)
    gate_pre = jnp.dot(portion, gate_local, preferred_element_type=F32)
    up_pre = jnp.dot(portion, up_local, preferred_element_type=F32)
    logistic = jax.nn.sigmoid(gate_pre)
    activated = gate_pre * logistic
    derivative = logistic * (1.0 + gate_pre * (1.0 - logistic))
    hidden = (activated * up_pre).astype(BF16)
    outputs = jnp.dot(
        lax.all_gather(hidden, "node", axis=1, tiled=True),
        down_local,
        preferred_element_type=F32,
    ).astype(BF16)
    picked = exchange(outputs)[target_row].astype(F32)
    layer_out = jnp.sum(combine_weights[:, :, None] * picked, axis=1).astype(BF16)
    gate_terms = jnp.sum(cotangent.astype(F32)[:, None, :] * picked, axis=2)
    grad_gates = lax.psum(gate_terms, "node")
    hidden_terms = lax.dot_general(
        exchange(weighted), down_local, BACK_DIMS, preferred_element_type=F32
    )
    hidden_grad = lax.psum_scatter(
        hidden_terms.astype(BF16), "node", scatter_dimension=1, tiled=True
    ).astype(F32)
    gate_grad = (hidden_grad * up_pre * derivative).astype(BF16)
    up_grad = (hidden_grad * activated).astype(BF16)
    input_terms = lax.dot_general(gate_grad, gate_local, BACK_DIMS, preferred_element_type=F32)
    input_terms = input_terms + lax.dot_general(
        up_grad, up_local, BACK_DIMS, preferred_element_type=F32
    )
    summed = lax.psum_scatter(
        input_terms.astype(BF16), "node", scatter_dimension=1, tiled=True
    )
    grad_tokens = jnp.dot(spread, exchange(summed), preferred_element_type=F32).astype(BF16)
    return (layer_out, grad_tokens, grad_gates)


def swap(value, axis):
    return lax.ppermute(value, axis, [(0, 1), (1, 0)])


def shift(value, step):
    count = lax.axis_size("ep")
    return lax.ppermute(value, "ep", [(i, (i + step) % count) for i in range(count)])


def token_ordered(
    quantized, scales, expert_ids, combine_weights, gate_weight, up_weight, down_weight, cotangent
):
    ep_count = lax.axis_size("ep")
    me = lax.axis_index("ep")
    tok_count = expert_ids.shape[0]
    aligned = lax.axis_index("node") == lax.axis_index("sub")

    def dot(a, b):
        return jnp.dot(a, b, preferred_element_type=F32)

    def dot_back(a, b):
        return lax.dot_general(a, b, BACK_DIMS, preferred_element_type=F32)

    def order(a, b):
        return jnp.where(aligned, a, b), jnp.where(aligned, b, a)

    widened = jnp.repeat(scales, BLOCK, axis=1)
    tokens = (quantized.astype(F32) * widened).astype(BF16)

    def weight_for(expert):
        return jnp.sum(jnp.where(expert_ids == expert, combine_weights, 0.0), axis=1)

    row_weight = [weight_for(me)]
    for k in range(1, ep_count):
        row_weight.append(shift(weight_for((me + k) % ep_count), k))
    row_weight = jnp.concatenate(row_weight)[:, None]

    pieces, others = [tokens], []
    for k in range(ep_count):
        others.append(swap(pieces[k], "node"))
        if k + 1 < ep_count:
            pieces.append(shift(pieces[k], 1))
    grads = [cotangent]
    for k in range(1, ep_count):
        grads.append(shift(grads[-1], 1))
    gate_own, up_own, down_own = gate_weight[0], up_weight[0], down_weight[0]
    gate_far, up_far, down_far = swap(gate_own, "sub"), swap(up_own, "sub"), swap(down_own, "sub")

    near, far = order(jnp.concatenate(pieces), jnp.concatenate(others))
    gate_pre = dot(near, gate_own) + dot(far, gate_far)
    up_pre = dot(near, up_own) + dot(far, up_far)
    logistic = jax.nn.sigmoid(gate_pre)
    activated = gate_pre * logistic
    derivative = logistic * (1.0 + gate_pre * (1.0 - logistic))
    hidden = activated * up_pre
    hidden_weighted = (hidden * row_weight).astype(BF16)
    hidden_near, hidden_far = order(hidden_weighted, swap(hidden_weighted, "node"))
    terms = (dot(hidden_near, down_own) + dot(hidden_far, down_far)).astype(BF16)
    layer_out = terms[:tok_count].astype(F32)
    for k in range(1, ep_count):
        layer_out += shift(terms[k * tok_count : (k + 1) * tok_count], -k).astype(F32)

    grad_rows = jnp.concatenate(grads)
    kept, sent = order(dot_back(grad_rows, down_own), dot_back(grad_rows, down_far))
    hidden_grad = kept + swap(sent.astype(BF16), "node").astype(F32)
    gate_sum = jnp.sum(hidden * hidden_grad, axis=1)
    gate_sum = gate_sum + swap(gate_sum, "node")
    grad_gates = jnp.zeros(expert_ids.shape, F32)
    for k in range(ep_count):
        part = gate_sum[k * tok_count : (k + 1) * tok_count]
        part = shift(part, -k) if k else part
        grad_gates += jnp.where(expert_ids == (me + k) % ep_count, part[:, None], 0.0)

    hidden_grad = hidden_grad * row_weight
    gate_grad = (hidden_grad * up_pre * derivative).astype(BF16)
    up_grad = (hidden_grad * activated).astype(BF16)
    input_kept, input_sent = order(
        dot_back(gate_grad, gate_own) + dot_back(up_grad, up_own),
        dot_back(gate_grad, gate_far) + dot_back(up_grad, up_far),
    )
    input_sent = input_sent.astype(BF16)
    grad_tokens = None
    for k in [*range(1, ep_count), 0]:
        rows = slice(k * tok_count, (k + 1) * tok_count)
        part = input_kept[rows] + swap(input_sent[rows], "node").astype(F32)
        part = shift(part.astype(BF16), -k).astype(F32) if k else part
        grad_tokens = part if grad_tokens is None else grad_tokens + part
    return (layer_out.astype(BF16), grad_tokens.astype(BF16), grad_gates)


def solution(mesh):
    def per_device(*args):
        tok_count, top_count = args[2].shape
        ep_count = lax.axis_size("ep")
        unpacked = 2 * top_count >= ep_count
        pairs = lax.axis_size("node") == 2 and lax.axis_size("sub") == 2
        return (token_ordered if unpacked and pairs else slotted)(*args)

    return jax.shard_map(
        per_device,
        mesh=mesh,
        in_specs=(
            P(("groups", "ep", "sub"), "node"),
            P(("groups", "ep", "sub"), "node"),
            P(("groups", "ep", "sub"), None),
            P(("groups", "ep", "sub"), None),
            P("ep", "sub", "node"),
            P("ep", "sub", "node"),
            P("ep", "sub", "node"),
            P(("groups", "ep", "sub"), "node"),
        ),
        out_specs=(
            P(("groups", "ep", "sub"), "node"),
            P(("groups", "ep", "sub"), "node"),
            P(("groups", "ep", "sub"), None),
        ),
        check_vma=False,
    )
```
